32 devices in a mesh: layer: 2 (over core), latent: 16 (over z, y, x).
Axes of the slice: x: 2, y: 2, z: 4, core: 2. Of those that a mesh axis runs over, the one named last changes fastest.
Arguments:
- activations: bfloat16 [2, 512, 2048], P('layer', 'latent'), may hold values from -15 to 15
- enc_weight: bfloat16 [2, 2048, 16384], P('layer', None, 'latent'), may hold values from -0.09375 to 0.09375
- enc_bias: float32 [16384], P('latent'), may hold values from -3 to 3
- dec_weight: bfloat16 [2, 16384, 2048], P('layer', 'latent'), may hold values from -0.1796875 to 0.1796875
- dec_bias: float32 [2, 2048], P('layer'), may hold values from -3 to 3
- active_mask: int32 [512, 16384], P(None, 'latent'), may hold values 0 or 1
Outputs:
- grad_enc: bfloat16 [2, 2048, 16384], P('layer', None, 'latent')
- grad_dec: bfloat16 [2, 16384, 2048], P('layer', 'latent')
- loss_value: float32 [], replicated
The draws below stay inside these ranges and needn't reach their ends.
All inputs are finite; a program needn't handle non-finite values. No bound on the sum of `active_mask` on one device may be relied on, other than what follows from the above.
Results may differ from the reference program's by a relative error of at most 0.0065.
Values may be sent and summed in bfloat16 or wider, within the bound.
A program may use at most 128 MiB of HBM per device.

```python
import jax
import jax.numpy as jnp
from jax import lax

D = 2048
TOK = 512
LAYERS = 2
LATENTS = 16384


def draw_activations(key, part):
    first = jax.random.fold_in(key, 0)
    layer_scale = 1.0 + 0.8 * jnp.arange(LAYERS, dtype=jnp.float32)[:, None, None] / max(LAYERS - 1, 1)
    base = jnp.clip(jax.random.normal(first, (LAYERS, TOK, D), jnp.float32), -7.0, 7.0)
    values = base * layer_scale
    return values.astype(jnp.bfloat16)


def draw_dec_weight(key, part):
    first = jax.random.fold_in(key, 0)
    rising = 3.0 ** (jnp.arange(LATENTS, dtype=jnp.float32) / LATENTS)
    layer_scale = 1.0 + 0.8 * jnp.arange(LAYERS, dtype=jnp.float32)[:, None, None] / max(LAYERS - 1, 1)
    factor = (2.0 * LATENTS) ** (-0.5)
    base = jnp.clip(jax.random.normal(first, (LAYERS, LATENTS, D), jnp.float32), -6.0, 6.0)
    values = base * rising[None, :, None] * layer_scale * factor
    return values.astype(jnp.bfloat16)


def touch_ends(array, stream_key, smallest, top_value):
    dims = array.shape
    place = [jax.random.randint(jax.random.fold_in(stream_key, axis), (), 0, dims[axis]) for axis in range(len(dims))]
    array = array.at[tuple(place)].set(smallest)
    longest = dims.index(max(dims))
    place[longest] = (place[longest] + 1) % dims[longest]
    return array.at[tuple(place)].set(top_value)


def block_scale(key, dims, shards, least, largest):
    factor_of = 1.0
    for position, blocks in shards:
        heights = jax.random.uniform(jax.random.fold_in(jax.random.fold_in(key, 6), position), (blocks,), jnp.float32, least / len(shards), largest / len(shards))
        factor_of = factor_of * jnp.repeat(jnp.exp(heights), dims[position] // blocks).reshape((-1,) + (1,) * (len(dims) - 1 - position))
    return factor_of


def scatter_about(rng, shape, width, limit, cuts=(), kind=jnp.bfloat16):
    drawn = jax.random.normal(rng, shape, jnp.float32) * width
    if len(cuts) > 0:
        drawn = block_scale(rng, shape, cuts, -0.22, 0.18) * drawn
    return jnp.clip(drawn, min=-limit, max=limit).astype(kind)


def setup_inputs(seed: int = 0) -> dict:
    streams_of = jax.random.split(jax.random.key(seed), 7)
    return {
        "activations": draw_activations(jax.random.fold_in(streams_of[6], 71), 0),
        "enc_weight": scatter_about(streams_of[1], (LAYERS, D, LATENTS), (LAYERS * D) ** -0.5, 0.09375, ((0, 2), (2, 16))),
        "enc_bias": scatter_about(streams_of[2], (LATENTS,), 0.5, 3.0, ((0, 16),), jnp.float32),
        "dec_weight": draw_dec_weight(jax.random.fold_in(streams_of[6], 71), 0),
        "dec_bias": scatter_about(streams_of[4], (LAYERS, D), 0.5, 3.0, ((0, 2),), jnp.float32),
        "active_mask": touch_ends((jax.random.randint(streams_of[5], (TOK, LATENTS), 0, 4) < 1).astype(jnp.int32), jax.random.fold_in(streams_of[5], 1), 0, 1),
    }


sparsity_weight = 0.4

def reference(activations, enc_weight, enc_bias, dec_weight, dec_bias, active_mask):
    preact = jnp.zeros((TOK, LATENTS), jnp.float32)
    for layer in range(LAYERS):
        preact = preact + jnp.dot(activations[layer], enc_weight[layer], preferred_element_type=jnp.float32)
    preact = preact + enc_bias
    gating = active_mask.astype(jnp.float32)
    latent_code = preact * gating
    code_b = latent_code.astype(jnp.bfloat16)
    norm_list = []
    for layer in range(LAYERS):
        dec_float = dec_weight[layer].astype(jnp.float32)
        norm_list.append(jnp.sqrt(lax.optimization_barrier(jnp.sum(dec_float * dec_float, axis=1)) + 1e-06))
    norm_sum = norm_list[0]
    for layer in range(1, LAYERS):
        norm_sum = norm_sum + norm_list[layer]
    square_part = jnp.float32(0.0)
    error_list = []
    code_grad = jnp.zeros((TOK, LATENTS), jnp.float32)
    for layer in range(LAYERS):
        recon = jnp.dot(code_b, dec_weight[layer], preferred_element_type=jnp.float32) + dec_bias[layer]
        error_full = recon - activations[layer].astype(jnp.float32)
        square_part = square_part + 0.5 * jnp.sum(error_full * error_full)
        error_b = error_full.astype(jnp.bfloat16)
        error_list.append(error_b)
        code_grad = code_grad + jnp.dot(error_b, dec_weight[layer].T, preferred_element_type=jnp.float32)
    code_grad = code_grad + sparsity_weight * norm_sum
    preact_grad = (code_grad * gating).astype(jnp.bfloat16)
    code_total = lax.optimization_barrier(jnp.sum(latent_code, axis=0))
    enc_list = []
    dec_list = []
    for layer in range(LAYERS):
        enc_list.append(jnp.dot(activations[layer].T, preact_grad, preferred_element_type=jnp.float32).astype(jnp.bfloat16))
        dec_float = dec_weight[layer].astype(jnp.float32)
        shrink = sparsity_weight * code_total[:, None] * dec_float / norm_list[layer][:, None]
        dec_list.append((jnp.dot(code_b.T, error_list[layer], preferred_element_type=jnp.float32) + shrink).astype(jnp.bfloat16))
    sparse_part = sparsity_weight * jnp.sum(latent_code * norm_sum)
    loss_value = (square_part + sparse_part) / (TOK * D)
    return (jnp.stack(enc_list), jnp.stack(dec_list), loss_value)
```

```python
import functools

import jax
import jax.numpy as jnp
from jax import lax
from jax.experimental import pallas as pl
from jax.experimental.pallas import tpu as pltpu
from jax.sharding import PartitionSpec as P

sparsity_weight = 0.4
MESH = pl.DeviceIdType.MESH
F32 = jnp.float32
BF16 = jnp.bfloat16


def plain_step(activations, enc_weight, enc_bias, dec_weight, dec_bias, active_mask):
    local_rows = activations[0]
    encoder = enc_weight[0]
    decoder = dec_weight[0]
    token_all = lax.all_gather(local_rows, "latent", axis=0, tiled=True)
    layer_pre = jnp.dot(token_all, encoder, preferred_element_type=jnp.float32)
    dec_float = decoder.astype(jnp.float32)
    row_norm = jnp.sqrt(jnp.sum(dec_float * dec_float, axis=1) + 1e-06)
    preact, norm_sum = lax.psum((layer_pre, row_norm), "layer")
    preact = preact + enc_bias
    gating = active_mask.astype(jnp.float32)
    latent_code = preact * gating
    code_b = latent_code.astype(jnp.bfloat16)
    layer_index = lax.axis_index("layer")
    recon_share = (
        lax.psum_scatter(
            jnp.dot(code_b, decoder, preferred_element_type=jnp.float32),
            "latent",
            scatter_dimension=0,
            tiled=True,
        )
        + dec_bias[0]
    )
    error_share = recon_share - local_rows.astype(jnp.float32)
    square_part = 0.5 * jnp.sum(error_share * error_share)
    error_b = lax.all_gather(error_share.astype(jnp.bfloat16), "latent", axis=0, tiled=True)
    layer_grad = jnp.einsum("td,fd->tf", error_b, decoder, preferred_element_type=jnp.float32)
    code_grad = lax.psum(layer_grad, "layer") + sparsity_weight * norm_sum
    preact_grad = (code_grad * gating).astype(jnp.bfloat16)
    grad_enc = jnp.einsum(
        "td,tf->df", token_all, preact_grad, preferred_element_type=jnp.float32
    ).astype(jnp.bfloat16)
    code_total = jnp.sum(latent_code, axis=0)
    shrink = sparsity_weight * code_total[:, None] * dec_float / row_norm[:, None]
    grad_dec = (
        jnp.einsum("tf,td->fd", code_b, error_b, preferred_element_type=jnp.float32) + shrink
    ).astype(jnp.bfloat16)
    sparse_part = jnp.where(
        layer_index == 0, sparsity_weight * jnp.sum(latent_code * norm_sum), 0.0
    )
    loss_total = lax.psum(square_part + sparse_part, ("layer", "latent"))
    loss_value = loss_total / (active_mask.shape[0] * token_all.shape[1])
    return (grad_enc[None], grad_dec[None], loss_value)


def exchange_kernel(n, group, act, enc_hbm, bias, dec_hbm, dbias, mask_hbm,
                    tok_t_out, code_t_out, err_out, pg_out, coef, loss_out,
                    enc, dec, mask, tok, tok_t, own, pre_send, pre_recv, code, code_t,
                    rs_send, rs_recv, err, lg_send, lg_recv, pg,
                    norm_own, norm_recv, total, loss_send, loss_recv, pair_send, pair_recv,
                    load_sem, out_sem, ag_s, ag_r, rs_s, rs_r, er_s, er_r, ls_s, ls_r,
                    pre_s, pre_r, lg_s, lg_r, nm_s, nm_r, pl_s, pl_r):
    me = lax.axis_index("latent")
    layer = lax.axis_index("layer")
    other = 1 - layer
    rows, width = act.shape
    tokens, latents = mask.shape
    span = group * rows
    groups = n // group
    mine = me // group
    spot = lax.rem(me, group)

    def place(step):
        half = (step + 1) // 2
        shift = jnp.where(lax.rem(step, 2) == 1, half, groups - half)
        return lax.rem(mine + shift, groups)

    def peer(index):
        return place(index // group) * group + lax.rem(spot + lax.rem(index, group), group)

    loads = [
        pltpu.make_async_copy(hbm, vmem, load_sem.at[i])
        for i, (hbm, vmem) in enumerate(((dec_hbm, dec), (enc_hbm, enc), (mask_hbm, mask)))
    ]
    for load in loads:
        load.start()

    barrier = pltpu.get_barrier_semaphore()

    def greet(index, carry):
        pl.semaphore_signal(barrier, inc=1, device_id={"latent": peer(index)}, device_id_type=MESH)
        return carry

    lax.fori_loop(1, n, greet, 0)
    pl.semaphore_signal(barrier, inc=1, device_id={"layer": other}, device_id_type=MESH)
    pl.semaphore_wait(barrier, n)

    def latent_copy(src, dst, send, recv, target):
        return pltpu.make_async_remote_copy(
            src_ref=src, dst_ref=dst, send_sem=send, recv_sem=recv,
            device_id={"latent": target}, device_id_type=MESH)

    def layer_copy(src, dst, send, recv):
        return pltpu.make_async_remote_copy(
            src_ref=src, dst_ref=dst, send_sem=send, recv_sem=recv,
            device_id={"layer": other}, device_id_type=MESH)

    def token_send(target):
        return latent_copy(act, tok.at[me], ag_s.at[target], ag_r.at[me], target)

    def token_recv(source):
        return latent_copy(act, tok.at[source], ag_s.at[source], ag_r.at[source], source)

    def each_peer(do):
        def body(index, carry):
            do(peer(index))
            return carry
        lax.fori_loop(1, n, body, 0)

    each_peer(lambda t: token_send(t).start())
    tok[me] = act[...]

    loads[0].wait()
    lanes = 128

    def norm_block(block, carry):
        at = pl.multiple_of(block * lanes, lanes)
        piece = dec[pl.ds(at, lanes), :].astype(F32)
        sums = jnp.sum(piece * piece, axis=1, keepdims=True)
        norm = jnp.sqrt(sums + 1e-06)
        norm_own[:, pl.ds(at, lanes)] = jnp.broadcast_to(norm, (lanes, lanes)).T[0:8, :]
        return carry

    lax.fori_loop(0, latents // lanes, norm_block, 0)
    norm_copy = layer_copy(norm_own, norm_recv, nm_s, nm_r)
    norm_copy.start()
    total[...] = jnp.zeros_like(total)
    loads[1].wait()
    loads[2].wait()

    def rows_of(g):
        return pl.ds(pl.multiple_of(g * span, span), span)

    def pre_copy(g):
        return layer_copy(pre_send.at[g], pre_recv.at[g], pre_s.at[g], pre_r.at[g])

    def lg_copy(g):
        return layer_copy(lg_send.at[g], lg_recv.at[g], lg_s.at[g], lg_r.at[g])

    def rs_copy(target):
        return latent_copy(rs_send.at[target], rs_recv.at[me], rs_s.at[target], rs_r.at[me], target)

    def rs_wait(source):
        return latent_copy(rs_send.at[source], rs_recv.at[source], rs_s.at[source], rs_r.at[source], source)

    def wait_group(step, make):
        def body(j, carry):
            source = peer(step * group + j)

            @pl.when(source != me)
            def _():
                make(source).wait_recv()
            return carry
        lax.fori_loop(0, group, body, 0)

    tile = min(512, latents)
    wide = min(512, width)

    def encode(step):
        g = place(step)
        wait_group(step, token_recv)
        left = tok[pl.ds(g * group, group)].reshape(span, width)
        for c in range(latents // tile):
            cols = pl.ds(c * tile, tile)
            part = jnp.dot(left, enc[:, cols], preferred_element_type=F32)
            own[rows_of(g), cols] = part
            pre_send[g, :, cols] = part.astype(BF16)
        pre_copy(g).start()
        tok_t[:, rows_of(g)] = left.T

    def decode(step):
        g = place(step)
        pre_copy(g).wait_recv()
        here = rows_of(g)
        for c in range(latents // tile):
            cols = pl.ds(c * tile, tile)
            preact = own[here, cols] + pre_recv[g, :, cols].astype(F32) + bias[0:1, cols]
            latent = preact * mask[here, cols].astype(F32)
            total[0:1, cols] += jnp.sum(latent, axis=0, keepdims=True)
            code[:, cols] = latent.astype(BF16)
        left = code[...]
        for c in range(width // wide):
            cols = pl.ds(c * wide, wide)
            part = jnp.dot(left, dec[:, cols], preferred_element_type=F32).astype(BF16)
            rs_send[pl.ds(g * group, group), :, cols] = part.reshape(group, rows, wide)

        def send(j, carry):
            target = peer(step * group + j)

            @pl.when(target != me)
            def _():
                rs_copy(target).start()
            return carry

        lax.fori_loop(0, group, send, 0)
        code_t[:, here] = left.T

    def forward(step, carry):
        @pl.when(step < groups)
        def _():
            encode(step)

        @pl.when(step > 0)
        def _():
            decode(step - 1)
        return carry

    lax.fori_loop(0, groups + 1, forward, 0)

    outs = [
        pltpu.make_async_copy(vmem, hbm, out_sem.at[i])
        for i, (vmem, hbm) in enumerate(
            ((tok_t, tok_t_out), (code_t, code_t_out), (err, err_out), (pg, pg_out)))
    ]
    outs[0].start()
    outs[1].start()

    norm_copy.wait()
    norm_sum = norm_own[0:1, :] + norm_recv[0:1, :]
    sparse = sparsity_weight * jnp.sum(total[0:1, :] * norm_sum)
    ratio = sparsity_weight * total[0:1, :] / norm_own[0:1, :]
    coef[...] = jnp.broadcast_to(ratio, (128, latents)).T
    norm_recv[...] = jnp.broadcast_to(sparsity_weight * norm_sum, norm_recv.shape)

    rs_recv[me] = rs_send[me]
    each_peer(lambda s: rs_wait(s).wait_recv())
    squares = jnp.zeros((1, 1), F32)
    for c in range(width // wide):
        cols = pl.ds(c * wide, wide)
        recon = rs_recv[0, :, cols].astype(F32)
        for s in range(1, n):
            recon = recon + rs_recv[s, :, cols].astype(F32)
        error = recon + dbias[0:1, cols] - act[:, cols].astype(F32)
        squares = squares + jnp.sum(error * error)
        err[me, :, cols] = error.astype(BF16)
    partial = 0.5 * squares + jnp.where(layer == 0, sparse, 0.0)
    loss_send[...] = jnp.broadcast_to(partial, loss_send.shape)
    loss_recv[me] = loss_send[...]

    def err_send(target):
        return latent_copy(err.at[me], err.at[me], er_s.at[target], er_r.at[me], target)

    def err_recv(source):
        return latent_copy(err.at[source], err.at[source], er_s.at[source], er_r.at[source], source)

    def loss_copy(target):
        return latent_copy(loss_send, loss_recv.at[me], ls_s.at[target], ls_r.at[me], target)

    def loss_wait(source):
        return latent_copy(loss_send, loss_recv.at[source], ls_s.at[source], ls_r.at[source], source)

    each_peer(lambda t: err_send(t).start())
    each_peer(lambda t: loss_copy(t).start())

    def grad(step):
        g = place(step)
        wait_group(step, err_recv)
        left = err[pl.ds(g * group, group)].reshape(span, width)
        for c in range(latents // tile):
            part = lax.dot_general(
                left, dec[pl.ds(c * tile, tile), :], (((1,), (1,)), ((), ())),
                preferred_element_type=F32)
            cols = pl.ds(c * tile, tile)
            own[rows_of(g), cols] = part
            lg_send[g, :, cols] = part.astype(BF16)
        lg_copy(g).start()

    def gate(step):
        g = place(step)
        here = rows_of(g)
        lg_copy(g).wait_recv()
        for c in range(latents // tile):
            cols = pl.ds(c * tile, tile)
            code_grad = own[here, cols] + lg_recv[g, :, cols].astype(F32) + norm_recv[0:1, cols]
            pg[here, cols] = (code_grad * mask[here, cols].astype(F32)).astype(BF16)

    def backward(step, carry):
        @pl.when(step < groups)
        def _():
            grad(step)

        @pl.when(step > 0)
        def _():
            gate(step - 1)
        return carry

    lax.fori_loop(0, groups + 1, backward, 0)
    outs[2].start()
    outs[3].start()

    each_peer(lambda s: loss_wait(s).wait_recv())
    pair_send[...] = jnp.sum(loss_recv[...], axis=0)
    pair = layer_copy(pair_send, pair_recv, pl_s, pl_r)
    pair.start()

    def finish(target):
        token_send(target).wait_send()
        rs_copy(target).wait_send()
        err_send(target).wait_send()
        loss_copy(target).wait_send()

    each_peer(finish)

    def finish_pair(g, carry):
        pre_copy(g).wait_send()
        lg_copy(g).wait_send()
        return carry

    lax.fori_loop(0, groups, finish_pair, 0)
    pair.wait()
    loss_out[...] = (pair_send[...] + pair_recv[...]) / (tokens * width)
    for out in outs:
        out.wait()


def grads_kernel(tok_t, pg, code_t, err, dec, coef, enc_out, dec_out):
    enc_out[...] = jnp.dot(tok_t[...], pg[...], preferred_element_type=F32).astype(BF16)
    shrink = coef[:, 0:1] * dec[...].astype(F32)
    dec_out[...] = (jnp.dot(code_t[...], err[...], preferred_element_type=F32) + shrink).astype(BF16)


def fast_step(n, activations, enc_weight, enc_bias, dec_weight, dec_bias, active_mask):
    rows, width = activations.shape[1:]
    tokens, latents = active_mask.shape
    group = max(1, min(n, 128 // rows))
    groups = n // group
    span = group * rows
    decoder = dec_weight[0]
    vmem = pl.BlockSpec(memory_space=pltpu.VMEM)
    anyw = pl.BlockSpec(memory_space=pl.ANY)
    shape = jax.ShapeDtypeStruct
    dma = pltpu.SemaphoreType.DMA
    tok_t, code_t, err, pg, coef, loss = pl.pallas_call(
        functools.partial(exchange_kernel, n, group),
        out_shape=(
            shape((width, tokens), BF16),
            shape((latents, tokens), BF16),
            shape((n, rows, width), BF16),
            shape((tokens, latents), BF16),
            shape((latents, 128), F32),
            shape((8, 128), F32),
        ),
        in_specs=[vmem, anyw, vmem, anyw, vmem, anyw],
        out_specs=(anyw, anyw, anyw, anyw, vmem, vmem),
        scratch_shapes=[
            pltpu.VMEM((width, latents), BF16),
            pltpu.VMEM((latents, width), BF16),
            pltpu.VMEM((tokens, latents), jnp.int32),
            pltpu.VMEM((n, rows, width), BF16),
            pltpu.VMEM((width, tokens), BF16),
            pltpu.VMEM((tokens, latents), F32),
            pltpu.VMEM((groups, span, latents), BF16),
            pltpu.VMEM((groups, span, latents), BF16),
            pltpu.VMEM((span, latents), BF16),
            pltpu.VMEM((latents, tokens), BF16),
            pltpu.VMEM((n, rows, width), BF16),
            pltpu.VMEM((n, rows, width), BF16),
            pltpu.VMEM((n, rows, width), BF16),
            pltpu.VMEM((groups, span, latents), BF16),
            pltpu.VMEM((groups, span, latents), BF16),
            pltpu.VMEM((tokens, latents), BF16),
            pltpu.VMEM((8, latents), F32),
            pltpu.VMEM((8, latents), F32),
            pltpu.VMEM((8, latents), F32),
            pltpu.VMEM((8, 128), F32),
            pltpu.VMEM((n, 8, 128), F32),
            pltpu.VMEM((8, 128), F32),
            pltpu.VMEM((8, 128), F32),
            dma((3,)), dma((4,)),
            dma((n,)), dma((n,)), dma((n,)), dma((n,)), dma((n,)), dma((n,)), dma((n,)), dma((n,)),
            dma((groups,)), dma((groups,)), dma((groups,)), dma((groups,)),
            dma, dma, dma, dma,
        ],
        compiler_params=pltpu.CompilerParams(collective_id=0, has_side_effects=True),
    )(activations[0], enc_weight[0], enc_bias[None], decoder, dec_bias, active_mask)
    err = err.reshape(tokens, width)
    tile = min(256, latents)
    grad_enc, grad_dec = pl.pallas_call(
        grads_kernel,
        grid=(latents // tile,),
        out_shape=(shape((width, latents), BF16), shape((latents, width), BF16)),
        in_specs=[
            pl.BlockSpec((width, tokens), lambda i: (0, 0)),
            pl.BlockSpec((tokens, tile), lambda i: (0, i)),
            pl.BlockSpec((tile, tokens), lambda i: (i, 0)),
            pl.BlockSpec((tokens, width), lambda i: (0, 0)),
            pl.BlockSpec((tile, width), lambda i: (i, 0)),
            pl.BlockSpec((tile, 128), lambda i: (i, 0)),
        ],
        out_specs=(
            pl.BlockSpec((width, tile), lambda i: (0, i)),
            pl.BlockSpec((tile, width), lambda i: (i, 0)),
        ),
    )(tok_t, pg, code_t, err, decoder, coef)
    return (grad_enc[None], grad_dec[None], loss[0, 0])


def solution(mesh):
    placed = (
        P("layer", "latent", None),
        P("layer", None, "latent"),
        P("latent"),
        P("layer", "latent", None),
        P("layer", None),
        P(None, "latent"),
    )
    n = mesh.shape["latent"]

    def per_device(activations, *others):
        rows = activations.shape[1]
        if rows % 16 == 0 and 128 % rows == 0:
            return fast_step(n, activations, *others)
        return plain_step(activations, *others)

    return jax.shard_map(
        per_device,
        mesh=mesh,
        in_specs=placed,
        out_specs=(P("layer", None, "latent"), P("layer", "latent", None), P()),
        check_vma=False,
    )
```
